32 devices in a mesh: seq: 8 (over z, x), vocab: 4 (over y, core).
Axes of the slice: x: 2, y: 2, z: 4, core: 2. Of those that a mesh axis runs over, the one named last changes fastest.
Arguments:
- rollout: bfloat16 [288, 4096], P('seq')
- group_count: int32 [8], replicated, may hold values from 12 to 36, as said below
- final_gain: float32 [4096], replicated, may hold values from 0.5 to 1.5
- head_weight: bfloat16 [4096, 152064], P(None, ('seq', 'vocab'))
- teacher_index: int32 [192, 64], replicated, may hold values from 0 to 152063, as said below
- teacher_logprob: float32 [192, 64], replicated, as said below
Outputs:
- kl: float32 [192], P('seq')
- grad_weight: bfloat16 [4096, 152064], P(None, ('seq', 'vocab'))
- grad_rollout: bfloat16 [288, 4096], P('seq', 'vocab')
The draws below stay inside these ranges and needn't reach their ends.
Inputs may be any that keep to these rules, and one draw needn't show every extreme that they name: The first group_count[g] of the 36 slots of group g are live, the rest padding; the counts sum to 192. `teacher_index`: the 64 ids of one token are distinct. `teacher_logprob`: the exponentials of one token's entries sum to less than 1.
All inputs are finite; a program needn't handle non-finite values.
Results may differ from the reference program's by a relative error of at most 0.0075.
Values may be sent and summed in bfloat16 or wider, within the bound.
A program may use at most 128 MiB of HBM per device.

```python
import math
import jax
import jax.numpy as jnp
from jax import lax

D = 4096
VOCAB = 152064
TOPK = 64
PACK_DEV = 24
SLOT_DEV = 36
TOKENS = 192
GEN_SLOTS = 288
N_SEQ = 8


def drawn_columns(key):
    inner = jax.random.fold_in(key, 7)
    columns = 2 * jax.random.randint(jax.random.fold_in(inner, 1), (4,), 0, VOCAB // 2)
    vectors = jax.random.uniform(jax.random.fold_in(inner, 2), (4, D), jnp.float32, -1.0, 1.0) * math.sqrt(3.0)
    return (columns, vectors)


def draw_head_weight(key, part):
    spread = 3.5 / math.sqrt(D)
    table = jax.random.normal(key, (D, VOCAB), jnp.float32) * spread
    table = jnp.clip(table, -5.5 * spread, 5.5 * spread)
    columns, vectors = drawn_columns(key)
    strong = 320.0 / D * vectors.T
    table = table.at[:, columns].set(strong)
    table = table.at[:, columns + 1].set(0.993 * strong)
    return table.astype(jnp.bfloat16)


def draw_rollout(key, part):
    table = jax.random.normal(key, (GEN_SLOTS, D), jnp.float32)
    columns, vectors = drawn_columns(key)
    picker = jax.random.fold_in(key, 5)
    chosen_group = jax.random.randint(jax.random.fold_in(picker, 1), (8,), 0, GEN_SLOTS // SLOT_DEV)
    chosen_row = jax.random.randint(jax.random.fold_in(picker, 2), (8,), 0, PACK_DEV // 2)
    row_ids = chosen_group * SLOT_DEV + chosen_row
    strength = jnp.array([0.5, 1.0, 2.0, 4.0, 0.5, 1.0, 2.0, 4.0], jnp.float32)[:, None]
    which = jnp.arange(8) % 4
    table = table.at[row_ids].set(table[row_ids] + strength * vectors[which])
    return table.astype(jnp.bfloat16)


def draw_group_count(key, part):
    group_total = GEN_SLOTS // SLOT_DEV
    half_pack = PACK_DEV // 2
    group_order = jax.random.permutation(jax.random.fold_in(key, 11), group_total)
    shift_size = jax.random.randint(jax.random.fold_in(key, 12), (group_total // 2,), -(half_pack - 1), half_pack)
    shift_size = shift_size.at[0].set(half_pack)
    counts = jnp.zeros((group_total,), jnp.int32)
    counts = counts.at[group_order[0::2]].set(PACK_DEV + shift_size)
    counts = counts.at[group_order[1::2]].set(PACK_DEV - shift_size)
    return counts.astype(jnp.int32)


def draw_teacher_index(key, part):
    row_keys = jax.random.split(jax.random.fold_in(key, 21), TOKENS)
    residues = jax.vmap(lambda row_key: jax.random.permutation(row_key, TOPK))(row_keys)
    bucket = jax.random.randint(jax.random.fold_in(key, 22), (TOKENS, TOPK), 0, VOCAB // TOPK)
    return (bucket * TOPK + residues).astype(jnp.int32)


def draw_teacher_logprob(key, part):
    raw = 2.0 * jax.random.normal(key, (TOKENS, TOPK), jnp.float32)
    teacher_mass = jax.random.uniform(jax.random.fold_in(key, 31), (TOKENS, 1), jnp.float32, 0.5, 0.98)
    result = raw - jax.nn.logsumexp(raw, axis=1, keepdims=True) + jnp.log(teacher_mass)
    return result.astype(jnp.float32)


def setup_inputs(seed: int = 0) -> dict:
    keys = jax.random.split(jax.random.key(seed), 7)
    return {
        "rollout": draw_rollout(jax.random.fold_in(keys[6], 71), 0),
        "group_count": draw_group_count(jax.random.fold_in(keys[6], 71), 0),
        "final_gain": jnp.clip(1.0 + 0.1 * jax.random.normal(keys[2], (D,), jnp.float32), 0.5, 1.5),
        "head_weight": draw_head_weight(jax.random.fold_in(keys[6], 71), 0),
        "teacher_index": draw_teacher_index(jax.random.fold_in(keys[6], 71), 0),
        "teacher_logprob": draw_teacher_logprob(jax.random.fold_in(keys[6], 71), 0),
    }


norm_eps = 1e-06
loss_scale = 16.0

def pack_index(group_count):
    offsets = jnp.cumsum(group_count) - group_count
    row_ids = jnp.arange(SLOT_DEV, dtype=jnp.int32)
    rank = offsets[:, None] + row_ids[None, :]
    is_live = row_ids[None, :] < group_count[:, None]
    target = rank % N_SEQ * PACK_DEV + rank // N_SEQ
    target = jnp.where(is_live, target, TOKENS).astype(jnp.int32)
    return (target.reshape(-1), is_live.reshape(-1))

def reference(rollout, group_count, final_gain, head_weight, teacher_index, teacher_logprob):
    target, is_live = pack_index(group_count)
    packed = jnp.zeros((TOKENS, D), rollout.dtype).at[target].set(rollout, mode='drop')
    values = packed.astype(jnp.float32)
    inv_rms = lax.rsqrt(lax.optimization_barrier(jnp.mean(values * values, axis=1, keepdims=True)) + norm_eps)
    normed = (values * inv_rms * final_gain).astype(jnp.bfloat16)
    teacher_prob = jnp.exp(teacher_logprob)
    teacher_mass = lax.optimization_barrier(jnp.sum(teacher_prob, axis=1))
    block_width = VOCAB // 64
    block_ids = jnp.arange(64, dtype=jnp.int32)
    token_ids = jnp.arange(TOKENS, dtype=jnp.int32)[:, None]

    def block_logits(block_id):
        start = (block_id * block_width).astype(jnp.int32)
        weight_block = lax.dynamic_slice_in_dim(head_weight, start, block_width, 1)
        logits = jnp.dot(normed, weight_block, preferred_element_type=jnp.float32)
        local = teacher_index - start
        owned = (local >= 0) & (local < block_width)
        return (weight_block, logits, local, owned)

    def first_pass(carry, block_id):
        row_peak, row_total, target_sum = carry
        weight_block, logits, local, owned = block_logits(block_id)
        new_peak = jnp.maximum(row_peak, lax.optimization_barrier(jnp.max(logits, axis=1)))
        row_total = row_total * jnp.exp(row_peak - new_peak) + lax.optimization_barrier(jnp.sum(jnp.exp(logits - new_peak[:, None]), axis=1))
        picked = jnp.take_along_axis(logits, jnp.clip(local, 0, block_width - 1), axis=1)
        target_sum = target_sum + lax.optimization_barrier(jnp.sum(jnp.where(owned, teacher_prob * picked, 0.0), axis=1))
        return ((new_peak, row_total, target_sum), None)
    start_carry = (jnp.full((TOKENS,), -jnp.inf, jnp.float32), jnp.zeros((TOKENS,), jnp.float32), jnp.zeros((TOKENS,), jnp.float32))
    (row_peak, row_total, target_sum), _ = lax.scan(first_pass, start_carry, block_ids)
    log_total = row_peak + jnp.log(row_total)
    kl = lax.optimization_barrier(jnp.sum(teacher_prob * teacher_logprob, axis=1)) - target_sum + teacher_mass * log_total

    def second_pass(grad_normed, block_id):
        weight_block, logits, local, owned = block_logits(block_id)
        student_part = teacher_mass[:, None] * jnp.exp(logits - log_total[:, None])
        column = jnp.where(owned, local, block_width)
        student_part = student_part.at[token_ids, column].add(-teacher_prob, mode='drop')
        grad_logits = (loss_scale * student_part).astype(jnp.bfloat16)
        grad_block = lax.dot_general(normed, grad_logits, (((0,), (0,)), ((), ())), preferred_element_type=jnp.float32).astype(jnp.bfloat16)
        grad_normed = grad_normed + lax.dot_general(grad_logits, weight_block, (((1,), (1,)), ((), ())), preferred_element_type=jnp.float32)
        return (grad_normed, grad_block)
    grad_normed, grad_blocks = lax.scan(second_pass, jnp.zeros((TOKENS, D), jnp.float32), block_ids)
    grad_weight = grad_blocks.transpose(1, 0, 2).reshape(D, VOCAB)
    scaled_grad = grad_normed * final_gain
    row_dots = lax.optimization_barrier(jnp.sum(scaled_grad * values, axis=1, keepdims=True))
    grad_packed = ((scaled_grad - values * inv_rms * inv_rms * row_dots / D) * inv_rms).astype(jnp.bfloat16)
    gathered = jnp.take(grad_packed, jnp.minimum(target, TOKENS - 1), axis=0)
    grad_rollout = jnp.where(is_live[:, None], gathered, jnp.zeros_like(gathered))
    return (kl, grad_weight, grad_rollout)
```

```python
import functools

import jax
import jax.numpy as jnp
from jax import lax
from jax.experimental import pallas as pl
from jax.experimental.pallas import tpu as pltpu
from jax.sharding import PartitionSpec as P

norm_eps = 1e-06
loss_scale = 16.0
VMEM = pltpu.VMEM
DMA = pltpu.SemaphoreType.DMA


def remote(src, dst, send, recv, where):
    return pltpu.make_async_remote_copy(
        src_ref=src,
        dst_ref=dst,
        send_sem=send,
        recv_sem=recv,
        device_id=where,
        device_id_type=pl.DeviceIdType.MESH,
    )


def greet_all(groups, shares):
    s, v = lax.axis_index("seq"), lax.axis_index("vocab")
    barrier = pltpu.get_barrier_semaphore()
    for k in range(1, shares):
        pl.semaphore_signal(
            barrier, inc=1, device_id=(s, lax.rem(v + k, shares)), device_id_type=pl.DeviceIdType.MESH
        )
    for k in range(1, groups):
        pl.semaphore_signal(
            barrier, inc=1, device_id=(lax.rem(s + k, groups), v), device_id_type=pl.DeviceIdType.MESH
        )
    pl.semaphore_wait(barrier, groups + shares - 2)
    return s, v


def dense_kernel(width, col_ref, prob_ref, out_ref):
    rows, entries = col_ref.shape
    step = 1280
    for start in range(0, width, step):
        size = min(step, width - start)
        ids = lax.broadcasted_iota(jnp.int32, (rows, size), 1) + start
        acc = jnp.zeros((rows, size), jnp.float32)
        for j in range(entries):
            acc = jnp.where(ids == col_ref[:, j : j + 1], prob_ref[:, j : j + 1], acc)
        out_ref[:, start : start + size] = acc


def teacher_table(column, prob, width):
    tokens, entries = column.shape
    return pl.pallas_call(
        functools.partial(dense_kernel, width),
        grid=(tokens // 8,),
        out_shape=jax.ShapeDtypeStruct((tokens, width), jnp.float32),
        in_specs=[pl.BlockSpec((8, entries), lambda i: (i, 0))] * 2,
        out_specs=pl.BlockSpec((8, width), lambda i: (i, 0)),
        cost_estimate=pl.CostEstimate(
            flops=tokens * entries * width, bytes_accessed=tokens * width * 40, transcendentals=0
        ),
    )(column, prob)


def merge_stats(ref, count):
    peak = ref[0, 0:1, :]
    for i in range(1, count):
        peak = jnp.maximum(peak, ref[i, 0:1, :])
    total = jnp.zeros_like(peak)
    target = jnp.zeros_like(peak)
    for i in range(count):
        total = total + ref[i, 1:2, :] * jnp.exp(ref[i, 0:1, :] - peak)
        target = target + ref[i, 2:3, :]
    return peak, total, target


def put_stats(ref, stats):
    for i in range(3):
        ref[i : i + 1, :] = stats[i]


def stats_kernel(groups, shares, in_ref, out_ref, near, far, send_a, recv_a, send_b, recv_b):
    s, v = greet_all(groups, shares)
    first = []
    for k in range(1, shares):
        first.append(
            remote(in_ref, near.at[v], send_a.at[k], recv_a.at[k], (s, lax.rem(v + k, shares)))
        )
        first[-1].start()
    near[v] = in_ref[...]
    for copy in first:
        copy.wait()
    put_stats(out_ref, merge_stats(near, shares))
    far[s] = out_ref[...]
    second = []
    for k in range(1, groups):
        second.append(
            remote(far.at[s], far.at[s], send_b.at[k], recv_b.at[k], (lax.rem(s + k, groups), v))
        )
        second[-1].start()
    for copy in second:
        copy.wait()
    put_stats(out_ref, merge_stats(far, groups))


def exchange_stats(stats, groups, shares):
    return pl.pallas_call(
        functools.partial(stats_kernel, groups, shares),
        out_shape=jax.ShapeDtypeStruct(stats.shape, stats.dtype),
        in_specs=[pl.BlockSpec(memory_space=VMEM)],
        out_specs=pl.BlockSpec(memory_space=VMEM),
        scratch_shapes=[
            VMEM((shares,) + stats.shape, jnp.float32),
            VMEM((groups,) + stats.shape, jnp.float32),
            DMA((shares,)),
            DMA((shares,)),
            DMA((groups,)),
            DMA((groups,)),
        ],
        compiler_params=pltpu.CompilerParams(collective_id=0, has_side_effects=True),
    )(stats)


def hidden_kernel(
    groups, shares, part_ref, place_ref, x_ref, inv_ref, gain_ref, out_ref,
    pair_in, held, cross_in, spread, rows_in, dots, dots_in,
    send_a, recv_a, send_b, recv_b, send_c, recv_c, send_d, recv_d,
):
    s, v = greet_all(groups, shares)
    width = part_ref.shape[1] // shares
    chips = shares // 2
    y, core = v // 2, lax.rem(v, 2)
    partner = (s, v + 1 - 2 * core)

    def columns(chip, side):
        return pl.ds(pl.multiple_of((2 * chip + side) * width, 128), width)

    order = list(range(1, chips)) + [0]
    pair = {}
    for k in order:
        chip = lax.rem(y + k, chips)
        pair[k] = remote(
            part_ref.at[:, columns(chip, 1 - core)], pair_in.at[k], send_a.at[k], recv_a.at[k], partner
        )
        pair[k].start()
    cross = []
    for k in range(1, chips):
        chip = lax.rem(y + k, chips)
        pair[k].wait()
        mine = part_ref[:, columns(chip, core)].astype(jnp.float32)
        held[k] = (mine + pair_in[k].astype(jnp.float32)).astype(jnp.bfloat16)
        copy = remote(
            held.at[k], cross_in.at[k], send_b.at[k], recv_b.at[k], (s, 2 * chip + core)
        )
        copy.start()
        cross.append(copy)
    pair[0].wait()
    total = part_ref[:, columns(y, core)].astype(jnp.float32) + pair_in[0].astype(jnp.float32)
    for k in range(1, chips):
        cross[k - 1].wait()
        total = total + cross_in[k].astype(jnp.float32)
    total = total.astype(jnp.bfloat16)
    back = []
    for k in range(1, groups):
        group = lax.rem(s + k, groups)
        spread[k] = jnp.dot(
            place_ref[group], total, preferred_element_type=jnp.float32
        ).astype(jnp.bfloat16)
        copy = remote(spread.at[k], rows_in.at[k], send_c.at[k], recv_c.at[k], (group, v))
        copy.start()
        back.append(copy)
    grad = jnp.dot(place_ref[s], total, preferred_element_type=jnp.float32)
    for k in range(1, groups):
        back[k - 1].wait()
        grad = grad + rows_in[k].astype(jnp.float32)
    x = x_ref[...].astype(jnp.float32)
    inv = inv_ref[...]
    u = grad * gain_ref[...]
    own_dots = jnp.sum(u * x, axis=1, keepdims=True)
    dots[...] = jnp.broadcast_to(own_dots, dots.shape)
    last = []
    for k in range(1, shares):
        copy = remote(dots, dots_in.at[k], send_d.at[k], recv_d.at[k], (s, lax.rem(v + k, shares)))
        copy.start()
        last.append(copy)
    row_dots = own_dots
    for k in range(1, shares):
        last[k - 1].wait()
        row_dots = row_dots + dots_in[k][:, 0:1]
    features = width * shares
    out_ref[...] = ((u - x * inv * inv * row_dots / features) * inv).astype(jnp.bfloat16)


def reduce_hidden(part, place, x, inv, gain, groups, shares):
    tokens, features = part.shape
    slots, width = x.shape
    chips = shares // 2
    return pl.pallas_call(
        functools.partial(hidden_kernel, groups, shares),
        out_shape=jax.ShapeDtypeStruct((slots, width), jnp.bfloat16),
        in_specs=[pl.BlockSpec(memory_space=VMEM)] * 5,
        out_specs=pl.BlockSpec(memory_space=VMEM),
        scratch_shapes=[
            VMEM((chips, tokens, width), jnp.bfloat16),
            VMEM((chips, tokens, width), jnp.bfloat16),
            VMEM((chips, tokens, width), jnp.bfloat16),
            VMEM((groups, slots, width), jnp.bfloat16),
            VMEM((groups, slots, width), jnp.bfloat16),
            VMEM((slots, 128), jnp.float32),
            VMEM((shares, slots, 128), jnp.float32),
            DMA((chips,)),
            DMA((chips,)),
            DMA((chips,)),
            DMA((chips,)),
            DMA((groups,)),
            DMA((groups,)),
            DMA((shares,)),
            DMA((shares,)),
        ],
        compiler_params=pltpu.CompilerParams(
            collective_id=1, has_side_effects=True, vmem_limit_bytes=48 * 1024 * 1024
        ),
    )(part, place, x, inv, gain)


def per_device(rollout, group_count, final_gain, head_weight, teacher_index, teacher_logprob):
    groups, shares = lax.axis_size("seq"), lax.axis_size("vocab")
    slots, features = rollout.shape
    tokens = teacher_index.shape[0]
    pack_rows = tokens // groups
    vocab_dev = head_weight.shape[1]
    own_index = lax.axis_index("seq")

    all_slots = lax.all_gather(rollout, "seq", axis=0, tiled=True)

    first_column = lax.axis_index(("seq", "vocab")) * vocab_dev
    teacher_prob = jnp.exp(teacher_logprob)
    teacher_mass = jnp.sum(teacher_prob, axis=1)
    teacher_dense = teacher_table(teacher_index - first_column, teacher_prob, vocab_dev)

    group_ids = jnp.arange(groups, dtype=jnp.int32)
    offsets = jnp.sum(jnp.where(group_ids[None, :] < group_ids[:, None], group_count[None, :], 0), axis=1)
    slot_pad = -(-slots // 8) * 8
    row_ids = jnp.arange(slot_pad, dtype=jnp.int32)
    rank = offsets[:, None] + row_ids[None, :]
    is_live = row_ids[None, :] < group_count[:, None]
    target = jnp.where(is_live, rank % groups * pack_rows + rank // groups, -1)
    token_ids = jnp.arange(tokens, dtype=jnp.int32)
    place = (target[:, :, None] == token_ids[None, None, :]).astype(jnp.bfloat16)
    gather = (target[:, :slots].reshape(1, -1) == token_ids[:, None]).astype(jnp.bfloat16)

    packed = jnp.dot(gather, all_slots, preferred_element_type=jnp.float32)
    inv_rms = lax.rsqrt(jnp.mean(packed * packed, axis=1, keepdims=True) + norm_eps)
    all_rows = (packed * inv_rms * final_gain).astype(jnp.bfloat16)
    logits = jnp.dot(all_rows, head_weight, preferred_element_type=jnp.float32)
    target_part = jnp.sum(teacher_dense * logits, axis=1)
    local_peak = jnp.max(logits, axis=1)
    local_total = jnp.sum(jnp.exp(logits - local_peak[:, None]), axis=1)
    stats = jnp.concatenate(
        [local_peak[None], local_total[None], target_part[None], jnp.zeros((5, tokens), jnp.float32)], axis=0
    )
    stats = exchange_stats(stats, groups, shares)
    log_total = stats[0] + jnp.log(stats[1])
    kl_all = jnp.sum(teacher_prob * teacher_logprob, axis=1) - stats[2] + teacher_mass * log_total
    kl = lax.dynamic_slice_in_dim(kl_all, own_index * pack_rows, pack_rows)
    student_part = teacher_mass[:, None] * jnp.exp(logits - log_total[:, None]) - teacher_dense
    grad_logits = (loss_scale * student_part).astype(jnp.bfloat16)
    part = lax.dot_general(
        grad_logits, head_weight, (((1,), (1,)), ((), ())), preferred_element_type=jnp.float32
    ).astype(jnp.bfloat16)

    share = features // shares
    feature_start = lax.axis_index("vocab") * share
    own = jnp.pad(rollout, ((0, slot_pad - slots), (0, 0)))
    own_values = own.astype(jnp.float32)
    own_inv = lax.rsqrt(jnp.mean(own_values * own_values, axis=1, keepdims=True) + norm_eps)
    own_x = lax.dynamic_slice_in_dim(own, feature_start, share, 1)
    own_gain = lax.dynamic_slice_in_dim(final_gain, feature_start, share, 0)[None, :]
    grad_rollout = reduce_hidden(part, place, own_x, own_inv, own_gain, groups, shares)[:slots]
    grad_weight = lax.dot_general(
        all_rows, grad_logits, (((0,), (0,)), ((), ())), preferred_element_type=jnp.float32
    ).astype(jnp.bfloat16)
    return (kl, grad_weight, grad_rollout)


def solution(mesh):
    placed = (P("seq", None), P(), P(), P(None, ("seq", "vocab")), P(), P())
    return jax.shard_map(
        per_device,
        mesh=mesh,
        in_specs=placed,
        out_specs=(P("seq"), P(None, ("seq", "vocab")), P("seq", "vocab")),
        check_vma=False,
    )
```
